32 devices in a mesh: chan: 16 (over z, x, core), win: 2 (over y).
Axes of the slice: x: 2, y: 2, z: 4, core: 2. Of those that a mesh axis runs over, the one named last changes fastest.
Arguments:
- spectra: bfloat16 [8, 1024, 2, 2048], P('win', 'chan'), may hold values from -4.5 to 4.5
- owners: int32 [4], replicated, may hold values from 0 to 15
- blocks: int32 [4], replicated, may hold values from 0 to 3
- max_lag: int32 [4, 16, 1024], P(None, 'win', 'chan'), may hold values from 1 to 64
Outputs:
- correlations: float32 [4, 16, 1024, 128], P(None, 'win', 'chan')
The draws below stay inside these ranges and needn't reach their ends.
All inputs are finite; a program needn't handle non-finite values.
Results may differ from the reference program's by a relative error of at most 0.0034.
Values may be sent and summed in bfloat16 or wider, within the bound.
A program may use at most 128 MiB of HBM per device.

```python
import jax
import jax.numpy as jnp
from jax import lax

F = 2048
W_DEV = 4
SRC = 16
C_DEV = 64
STEPS = 4
LAGS = 128
CHANNELS = 1024
WINDOWS = 8
N_CHAN = 16
N_WIN = 2


def touch_ends(drawn, rng, smallest, top_value):
    longest = drawn.shape.index(max(drawn.shape))
    spots = []
    for shift in (0, 1):
        where = [jax.random.randint(jax.random.fold_in(rng, axis), (), 0, length) for axis, length in enumerate(drawn.shape)]
        where[longest] = (where[longest] + shift) % drawn.shape[longest]
        spots.append(tuple(where))
    return drawn.at[spots[0]].set(smallest).at[spots[1]].set(top_value)


def levels(stream_key, extent, pieces, low, top_value):
    gain = 1.0
    for dim, blocks in pieces:
        heights = jax.random.uniform(jax.random.fold_in(jax.random.fold_in(stream_key, 6), dim), (blocks,), jnp.float32, low / len(pieces), top_value / len(pieces))
        gain = gain * jnp.repeat(jnp.exp(heights), extent[dim] // blocks).reshape((-1,) + (1,) * (len(extent) - 1 - dim))
    return gain


def bell_draw(stream_key, shape, scale, limit, cuts=(), kind=jnp.bfloat16):
    array = jax.random.normal(stream_key, shape, jnp.float32) * scale
    if len(cuts) > 0:
        array = levels(stream_key, shape, cuts, -0.22, 0.18) * array
    return jnp.clip(array, min=-limit, max=limit).astype(kind)


def setup_inputs(seed: int = 0) -> dict:
    key_list = jax.random.split(jax.random.key(seed), 5)
    spectra = bell_draw(key_list[0], (WINDOWS, CHANNELS, 2, F), 0.7, 4.5, ((0, 2), (1, 16)))
    owners = touch_ends(jax.random.randint(key_list[1], (STEPS,), 0, N_CHAN), jax.random.fold_in(key_list[1], 1), 0, N_CHAN - 1).astype(jnp.int32)
    blocks = touch_ends(jax.random.randint(key_list[2], (STEPS,), 0, C_DEV // SRC), jax.random.fold_in(key_list[2], 1), 0, (C_DEV // SRC) - 1).astype(jnp.int32)
    max_lag = touch_ends(jax.random.randint(key_list[3], (STEPS, SRC, CHANNELS), 1, LAGS // 2 + 1), jax.random.fold_in(key_list[3], 1), 1, (LAGS // 2 + 1) - 1).astype(jnp.int32)
    return dict(spectra=spectra, owners=owners, blocks=blocks, max_lag=max_lag)


def lag_table(bin_count, lag_count, window_count):
    bins = jnp.arange(bin_count, dtype=jnp.int32)[:, None]
    offsets = jnp.arange(lag_count, dtype=jnp.int32)[None, :] - lag_count // 2
    phase = (bins * offsets % (2 * bin_count)).astype(jnp.float32) * (jnp.pi / bin_count)
    weight = jnp.where(bins == 0, 1.0, 2.0).astype(jnp.float32) / jnp.sqrt(jnp.float32(2.0 * bin_count * window_count))
    return jnp.concatenate([weight * jnp.cos(phase), -weight * jnp.sin(phase)], 0).astype(jnp.bfloat16)

def cross_spectra(source_block, receivers):
    a_real = source_block[:, :, 0].astype(jnp.float32)
    a_imag = source_block[:, :, 1].astype(jnp.float32)
    b_real = receivers[:, :, 0].astype(jnp.float32)
    b_imag = receivers[:, :, 1].astype(jnp.float32)
    real_part = jnp.einsum('wsf,wcf->scf', a_real, b_real) + jnp.einsum('wsf,wcf->scf', a_imag, b_imag)
    imag_part = jnp.einsum('wsf,wcf->scf', a_imag, b_real) - jnp.einsum('wsf,wcf->scf', a_real, b_imag)
    return jnp.stack([real_part, imag_part], 2).astype(jnp.bfloat16)

def reference(spectra, owners, blocks, max_lag):
    lag_matrix = lag_table(F, LAGS, W_DEV * N_WIN)
    grouped = spectra.reshape(N_WIN, W_DEV, N_CHAN, C_DEV, 2, F).transpose(2, 0, 1, 3, 4, 5)
    offsets = jnp.abs(jnp.arange(LAGS, dtype=jnp.int32) - LAGS // 2)
    results = []
    for step_index in range(STEPS):
        first_channel = (owners[step_index] * C_DEV + blocks[step_index] * SRC).astype(jnp.int32)
        source_all = lax.dynamic_slice_in_dim(spectra, first_channel, SRC, 1)
        source_groups = source_all.reshape(N_WIN, W_DEV, SRC, 2, F)

        def one_block(receivers):
            summed_parts = jnp.zeros((SRC, C_DEV, LAGS), jnp.float32)
            for group in range(N_WIN):
                cross_part = cross_spectra(source_groups[group], receivers[group])
                flat = cross_part.reshape(SRC * C_DEV, 2 * F)
                summed_parts = summed_parts + jnp.dot(flat, lag_matrix, preferred_element_type=jnp.float32).reshape(SRC, C_DEV, LAGS)
            return summed_parts
        blocked = lax.map(one_block, grouped)
        whole = blocked.transpose(1, 0, 2, 3).reshape(SRC, CHANNELS, LAGS)
        inside = offsets[None, None, :] <= max_lag[step_index][:, :, None]
        results.append(jnp.where(inside, whole, jnp.float32(0.0)))
    return jnp.stack(results)
```

```python
import functools

import jax
import jax.numpy as jnp
from jax import lax
from jax.experimental import pallas as pl
from jax.experimental.pallas import tpu as pltpu
from jax.sharding import PartitionSpec as P

SRC = 16
STEPS = 4
LAGS = 128
LANES = 128


def from_root(value, axis, source):
    kept = jnp.where(lax.axis_index(axis) == source, value, 0).astype(value.dtype)
    return lax.psum(kept, axis)


def lag_table(bin_count, lag_count, window_count):
    bins = jnp.arange(bin_count, dtype=jnp.int32)[:, None]
    offsets = jnp.arange(lag_count, dtype=jnp.int32)[None, :] - lag_count // 2
    phase = (bins * offsets % (2 * bin_count)).astype(jnp.float32) * (jnp.pi / bin_count)
    weight = jnp.where(bins == 0, 1.0, 2.0).astype(jnp.float32) / jnp.sqrt(
        jnp.float32(2.0 * bin_count * window_count)
    )
    return jnp.concatenate([weight * jnp.cos(phase), -weight * jnp.sin(phase)], 1).astype(
        jnp.bfloat16
    )


def step_kernel(src_ref, recv_ref, lag_ref, out_ref, cross, *, terms, run, receivers):
    groups, sources, width = src_ref.shape
    lane = lax.broadcasted_iota(jnp.int32, (run, width), 1) % run
    row = lax.broadcasted_iota(jnp.int32, (run, width), 0)
    keep = (lane == row).astype(jnp.float32)
    zero = jnp.zeros((LANES, LANES), jnp.bfloat16)

    def group_step(g, carry):
        base = pl.multiple_of(g * 2 * run, 2 * run)
        first = jnp.concatenate([recv_ref[i, pl.ds(base, run), :] for i in range(terms)], 0)
        second = jnp.concatenate(
            [recv_ref[i, pl.ds(base + run, run), :] for i in range(terms)], 0
        )
        weight = jnp.concatenate(
            [jnp.concatenate([first, zero], 1), jnp.concatenate([zero, second], 1)], 0
        )
        values = src_ref[g].astype(jnp.float32)
        rows = jnp.concatenate(
            [
                (jnp.broadcast_to(values[s : s + 1], (run, width)) * keep).astype(jnp.bfloat16)
                for s in range(sources)
            ],
            0,
        )
        made = jnp.dot(rows, weight, preferred_element_type=jnp.float32).astype(jnp.bfloat16)
        for s in range(sources):
            part = made[s * run : (s + 1) * run]
            cross[pl.ds(base, run), s * LANES : (s + 1) * LANES] = part[:, :LANES]
            cross[pl.ds(base + run, run), s * LANES : (s + 1) * LANES] = part[:, LANES:]
        return carry

    lax.fori_loop(0, groups, group_step, 0, unroll=2)

    for pair in range(sources // 2):
        block = jnp.dot(
            lag_ref[...],
            cross[:, pair * 2 * LANES : (pair + 1) * 2 * LANES],
            preferred_element_type=jnp.float32,
        )
        turned = block.T
        lags = turned.shape[1] // 2
        for k in range(2):
            top = k * LANES
            out_ref[2 * pair + k] = (
                turned[top : top + receivers, :lags]
                + turned[top + receivers : top + 2 * receivers, lags:]
            )


def correlate(sources, received, lag_rows, receivers, run):
    groups, count, width = sources.shape
    terms, bins, _ = received.shape
    lags = lag_rows.shape[0] // 2
    return pl.pallas_call(
        functools.partial(step_kernel, terms=terms, run=run, receivers=receivers),
        out_shape=jax.ShapeDtypeStruct((count, receivers, lags), jnp.float32),
        in_specs=[pl.BlockSpec(memory_space=pltpu.VMEM)] * 3,
        out_specs=pl.BlockSpec(memory_space=pltpu.VMEM),
        scratch_shapes=[pltpu.VMEM((bins, count * LANES), jnp.bfloat16)],
        compiler_params=pltpu.CompilerParams(vmem_limit_bytes=40 << 20),
        cost_estimate=pl.CostEstimate(
            flops=8 * count * receivers * bins * lags,
            bytes_accessed=2 * (sources.size + received.size + lag_rows.size)
            + 4 * count * receivers * lags,
            transcendentals=0,
        ),
    )(sources, received, lag_rows)


def body(spectra, owners, blocks, max_lag):
    window_count, channel_count, _, bin_count = spectra.shape
    group_count = lax.axis_size("win")
    terms = 2 * window_count
    run = LANES // terms
    groups = bin_count // (2 * run)
    lag_rows = lag_table(bin_count, LAGS, window_count * group_count).T

    laid = spectra.reshape(window_count, channel_count, 2, groups, 2, run)
    laid = laid.transpose(3, 1, 4, 0, 2, 5).reshape(groups, channel_count, 2 * LANES)

    turned = spectra.transpose(0, 2, 3, 1)
    real, imag = turned[:, 0], turned[:, 1]
    received = jnp.stack(
        [jnp.concatenate([real, -imag], -1), jnp.concatenate([imag, real], -1)], 1
    ).reshape(terms, bin_count, 2 * channel_count)

    def pick(step_index):
        return lax.dynamic_slice_in_dim(laid, blocks[step_index] * SRC, SRC, 1)

    def fetch(step_index):
        return from_root(pick(step_index), "chan", owners[step_index])

    incoming = [fetch(step_index) for step_index in range(STEPS)]

    def stack_step(source_all):
        made = correlate(source_all, received, lag_rows, channel_count, run)
        return lax.psum_scatter(made, "win", scatter_dimension=0, tiled=True)

    stacked = jnp.stack([stack_step(incoming[step_index]) for step_index in range(STEPS)])
    offsets = jnp.abs(jnp.arange(LAGS, dtype=jnp.int32) - LAGS // 2)
    inside = offsets[None, None, None, :] <= max_lag[:, :, :, None]
    return jnp.where(inside, stacked, jnp.float32(0.0))


def solution(mesh):
    return jax.shard_map(
        body,
        mesh=mesh,
        in_specs=(P("win", "chan", None, None), P(), P(), P(None, "win", "chan")),
        out_specs=P(None, "win", "chan", None),
        check_vma=False,
    )
```

```python
import functools

import jax
import jax.numpy as jnp
import numpy as np
from jax import lax
from jax.experimental import pallas as pl
from jax.experimental.pallas import tpu as pltpu
from jax.sharding import PartitionSpec as P

SRC = 16
STEPS = 4
LAGS = 128
LANES = 128


def lag_rows(bin_count, lag_count, window_count):
    bins = np.arange(bin_count, dtype=np.int64)[None, :]
    offsets = np.arange(lag_count, dtype=np.int64)[:, None] - lag_count // 2
    phase = (bins * offsets % (2 * bin_count)) * (np.pi / bin_count)
    weight = np.where(bins == 0, 1.0, 2.0) / np.sqrt(2.0 * bin_count * window_count)
    rows = np.concatenate([weight * np.cos(phase), -weight * np.sin(phase)], 0)
    return rows.astype(np.float32).astype(jnp.bfloat16)


def prepare_kernel(blocks_ref, spectra_ref, laid_ref, recv_ref, *, run):
    windows, _, _, bins = spectra_ref.shape
    steps, _, sources, _ = laid_ref.shape
    terms = 2 * windows
    block = lax.broadcasted_iota(jnp.int32, (sources, LANES), 1) // run

    def chunk_step(q, carry):
        at = pl.ds(pl.multiple_of(q * LANES, LANES), LANES)
        for w in range(windows):
            real = spectra_ref[w, 0, :, at].astype(jnp.float32)
            imag = spectra_ref[w, 1, :, at].astype(jnp.float32)
            recv_ref[2 * w, at, :] = jnp.concatenate([real, -imag], 0).T.astype(jnp.bfloat16)
            recv_ref[2 * w + 1, at, :] = jnp.concatenate([imag, real], 0).T.astype(jnp.bfloat16)
        for step in range(steps):
            first = pl.ds(pl.multiple_of(blocks_ref[step] * sources, sources), sources)
            tiles = [
                spectra_ref[i // 2, i % 2, first, at].astype(jnp.float32) for i in range(terms)
            ]
            gap = terms // 2
            while gap:
                high = (block // gap) % 2 == 1
                for i in range(terms):
                    if (i // gap) % 2 == 0:
                        low_tile, high_tile = tiles[i], tiles[i + gap]
                        tiles[i] = jnp.where(
                            high, pltpu.roll(high_tile, gap * run, 1), low_tile
                        )
                        tiles[i + gap] = jnp.where(
                            high, high_tile, pltpu.roll(low_tile, LANES - gap * run, 1)
                        )
                gap //= 2
            for i in range(terms // 2):
                laid_ref[step, q * (terms // 2) + i] = jnp.concatenate(
                    tiles[2 * i : 2 * i + 2], 1
                ).astype(jnp.bfloat16)
        return carry

    lax.fori_loop(0, bins // LANES, chunk_step, 0)


def prepare(spectra, blocks, steps, sources, run):
    windows, channels, _, bins = spectra.shape
    return pl.pallas_call(
        functools.partial(prepare_kernel, run=run),
        out_shape=(
            jax.ShapeDtypeStruct((steps, bins // (2 * run), sources, 2 * LANES), spectra.dtype),
            jax.ShapeDtypeStruct((2 * windows, bins, 2 * channels), spectra.dtype),
        ),
        in_specs=[
            pl.BlockSpec(memory_space=pltpu.SMEM),
            pl.BlockSpec(memory_space=pltpu.VMEM),
        ],
        out_specs=(pl.BlockSpec(memory_space=pltpu.VMEM), pl.BlockSpec(memory_space=pltpu.VMEM)),
        compiler_params=pltpu.CompilerParams(vmem_limit_bytes=32 << 20),
    )(blocks, spectra.transpose(0, 2, 1, 3))


def spread_kernel(
    owners_ref, own_ref, out_ref,
    from_core, half, from_cross, quarter, from_low, from_high, to_high, to_low,
    core_send, core_recv, cross_send, cross_recv, up_send, up_recv,
    down_send, down_recv, share_send, share_recv, last_send, last_recv,
    *, length,
):
    steps = own_ref.shape[0]
    me = lax.axis_index("chan")
    line, cross, core = me // 4, (me // 2) % 2, me % 2
    core_peer = me + 1 - 2 * core
    cross_peer = me + 2 - 4 * cross
    mine = 2 * core + cross
    theirs = 2 * core + 1 - cross
    has_low, has_high = line > 0, line < length - 1

    def remote(src, dst, send, recv, peer):
        return pltpu.make_async_remote_copy(
            src_ref=src, dst_ref=dst, send_sem=send, recv_sem=recv,
            device_id={"chan": peer}, device_id_type=pl.DeviceIdType.MESH,
        )

    def to_core(s):
        part = own_ref.at[s, pl.ds(2 * (1 - core), 2)]
        return remote(part, from_core.at[s], core_send.at[s], core_recv.at[s], core_peer)

    def to_cross(s):
        return remote(
            half.at[s, 1 - cross], from_cross.at[s], cross_send.at[s], cross_recv.at[s],
            cross_peer,
        )

    def go_up(s):
        return remote(to_high.at[s], from_low.at[s], up_send.at[s], up_recv.at[s], me + 4)

    def go_down(s):
        return remote(to_low.at[s], from_high.at[s], down_send.at[s], down_recv.at[s], me - 4)

    def share(s):
        ref = out_ref.at[s, mine]
        return remote(ref, ref, share_send.at[s], share_recv.at[s], cross_peer)

    def last(s, which, index):
        ref = out_ref.at[s, index]
        return remote(ref, ref, last_send.at[s, which], last_recv.at[s, which], core_peer)

    barrier = pltpu.get_barrier_semaphore()

    def greet(peer):
        pl.semaphore_signal(
            barrier, inc=1, device_id={"chan": peer}, device_id_type=pl.DeviceIdType.MESH
        )

    greet(core_peer)
    greet(cross_peer)

    @pl.when(has_low)
    def _():
        greet(me - 4)

    @pl.when(has_high)
    def _():
        greet(me + 4)

    pl.semaphore_wait(
        barrier, 2 + jnp.where(has_low, 1, 0) + jnp.where(has_high, 1, 0)
    )

    @pl.loop(0, steps)
    def _(s):
        to_core(s).start()

    @pl.loop(0, steps)
    def _(s):
        to_core(s).wait_recv()
        half[s] = lax.select(owners_ref[s] == me, own_ref[s, pl.ds(2 * core, 2)], from_core[s])
        to_cross(s).start()

    @pl.loop(0, steps)
    def _(s):
        to_cross(s).wait_recv()
        value = lax.select((owners_ref[s] // 2) % 2 == cross, half[s, cross], from_cross[s])
        quarter[s] = value

        @pl.when(line == 0)
        def _():
            to_high[s] = value
            go_up(s).start()

        @pl.when(line == length - 1)
        def _():
            to_low[s] = value
            go_down(s).start()

    def low_side(s):
        @pl.when(has_low)
        def _():
            go_up(s).wait_recv()
            to_high[s] = lax.select(owners_ref[s] // 4 == line, quarter[s], from_low[s])

            @pl.when(has_high)
            def _():
                go_up(s).start()

    def high_side(s):
        @pl.when(has_high)
        def _():
            go_down(s).wait_recv()
            to_low[s] = lax.select(owners_ref[s] // 4 == line, quarter[s], from_high[s])

            @pl.when(has_low)
            def _():
                go_down(s).start()

    def finish(s):
        share(s).wait_recv()
        last(s, 1, theirs).start()

    @pl.loop(0, steps)
    def _(s):
        @pl.when(line < length // 2)
        def _():
            low_side(s)
            high_side(s)

        @pl.when(line >= length // 2)
        def _():
            high_side(s)
            low_side(s)

        out_ref[s, mine] = lax.select(owners_ref[s] // 4 <= line, to_high[s], to_low[s])
        share(s).start()
        last(s, 0, mine).start()

        @pl.when(s > 0)
        def _():
            finish(s - 1)

    finish(steps - 1)

    @pl.loop(0, steps)
    def _(s):
        to_core(s).wait_send()
        to_cross(s).wait_send()
        share(s).wait_send()
        for which in range(2):
            last(s, which, mine).wait()

        @pl.when(has_high)
        def _():
            go_up(s).wait_send()

        @pl.when(has_low)
        def _():
            go_down(s).wait_send()


def spread(laid, owners):
    steps, groups, sources, width = laid.shape
    rows = groups * sources // 4
    dtype = laid.dtype
    piece = (steps, rows, width)
    out = pl.pallas_call(
        functools.partial(spread_kernel, length=lax.axis_size("chan") // 4),
        out_shape=jax.ShapeDtypeStruct((steps, 4, rows, width), dtype),
        in_specs=[
            pl.BlockSpec(memory_space=pltpu.SMEM),
            pl.BlockSpec(memory_space=pltpu.VMEM),
        ],
        out_specs=pl.BlockSpec(memory_space=pltpu.VMEM),
        scratch_shapes=[
            pltpu.VMEM((steps, 2, rows, width), dtype),
            pltpu.VMEM((steps, 2, rows, width), dtype),
        ]
        + [pltpu.VMEM(piece, dtype)] * 6
        + [pltpu.SemaphoreType.DMA((steps,))] * 10
        + [pltpu.SemaphoreType.DMA((steps, 2))] * 2,
        compiler_params=pltpu.CompilerParams(
            collective_id=0, has_side_effects=True, vmem_limit_bytes=32 << 20
        ),
    )(owners, laid.reshape(steps, 4, rows, width))
    return out.reshape(steps, groups, sources, width)


def step_kernel(src_ref, recv_ref, lag_ref, out_ref, cross, *, terms, run, receivers):
    groups, sources, width = src_ref.shape
    lane = lax.broadcasted_iota(jnp.int32, (run, width), 1) % run
    row = lax.broadcasted_iota(jnp.int32, (run, width), 0)
    keep = (lane == row).astype(jnp.float32)
    zero = jnp.zeros((LANES, LANES), jnp.bfloat16)

    def group_step(g, carry):
        base = pl.multiple_of(g * 2 * run, 2 * run)
        first = jnp.concatenate([recv_ref[i, pl.ds(base, run), :] for i in range(terms)], 0)
        second = jnp.concatenate(
            [recv_ref[i, pl.ds(base + run, run), :] for i in range(terms)], 0
        )
        weight = jnp.concatenate(
            [jnp.concatenate([first, zero], 1), jnp.concatenate([zero, second], 1)], 0
        )
        values = src_ref[g].astype(jnp.float32)
        rows = jnp.concatenate(
            [
                (jnp.broadcast_to(values[s : s + 1], (run, width)) * keep).astype(jnp.bfloat16)
                for s in range(sources)
            ],
            0,
        )
        made = jnp.dot(rows, weight, preferred_element_type=jnp.float32).astype(jnp.bfloat16)
        for s in range(sources):
            part = made[s * run : (s + 1) * run]
            cross[pl.ds(base, run), s * LANES : (s + 1) * LANES] = part[:, :LANES]
            cross[pl.ds(base + run, run), s * LANES : (s + 1) * LANES] = part[:, LANES:]
        return carry

    lax.fori_loop(0, groups, group_step, 0, unroll=2)

    for pair in range(sources // 2):
        block = jnp.dot(
            lag_ref[...],
            cross[:, pair * 2 * LANES : (pair + 1) * 2 * LANES],
            preferred_element_type=jnp.float32,
        )
        turned = block.T
        lags = turned.shape[1] // 2
        for k in range(2):
            top = k * LANES
            out_ref[2 * pair + k] = (
                turned[top : top + receivers, :lags]
                + turned[top + receivers : top + 2 * receivers, lags:]
            )


def correlate(sources, received, lag_rows, receivers, run):
    groups, count, width = sources.shape
    terms, bins, _ = received.shape
    lags = lag_rows.shape[0] // 2
    return pl.pallas_call(
        functools.partial(step_kernel, terms=terms, run=run, receivers=receivers),
        out_shape=jax.ShapeDtypeStruct((count, receivers, lags), jnp.float32),
        in_specs=[pl.BlockSpec(memory_space=pltpu.VMEM)] * 3,
        out_specs=pl.BlockSpec(memory_space=pltpu.VMEM),
        scratch_shapes=[pltpu.VMEM((bins, count * LANES), jnp.bfloat16)],
        compiler_params=pltpu.CompilerParams(vmem_limit_bytes=40 << 20),
        cost_estimate=pl.CostEstimate(
            flops=8 * count * receivers * bins * lags,
            bytes_accessed=2 * (sources.size + received.size + lag_rows.size)
            + 4 * count * receivers * lags,
            transcendentals=0,
        ),
    )(sources, received, lag_rows)


def body(spectra, owners, blocks, max_lag):
    window_count, channel_count, _, bin_count = spectra.shape
    group_count = lax.axis_size("win")
    run = LANES // (2 * window_count)
    table = jnp.asarray(lag_rows(bin_count, LAGS, window_count * group_count))
    laid, received = prepare(spectra, blocks, STEPS, SRC, run)
    incoming = spread(laid, owners)

    def stack_step(source_all):
        made = correlate(source_all, received, table, channel_count, run)
        if group_count == 2:
            kept = SRC // 2
            place = lax.axis_index("win")
            sent = lax.dynamic_slice_in_dim(made, (1 - place) * kept, kept, 0)
            other = lax.ppermute(sent, "win", [(0, 1), (1, 0)])
            return lax.dynamic_slice_in_dim(made, place * kept, kept, 0) + other
        return lax.psum_scatter(made, "win", scatter_dimension=0, tiled=True)

    stacked = jnp.stack([stack_step(incoming[step_index]) for step_index in range(STEPS)])
    offsets = jnp.abs(jnp.arange(LAGS, dtype=jnp.int32) - LAGS // 2)
    inside = offsets[None, None, None, :] <= max_lag[:, :, :, None]
    return jnp.where(inside, stacked, jnp.float32(0.0))


def solution(mesh):
    return jax.shard_map(
        body,
        mesh=mesh,
        in_specs=(P("win", "chan", None, None), P(), P(), P(None, "win", "chan")),
        out_specs=P(None, "win", "chan", None),
        check_vma=False,
    )
```

```python
import functools

import jax
import jax.numpy as jnp
import numpy as np
from jax import lax
from jax.experimental import pallas as pl
from jax.experimental.pallas import tpu as pltpu
from jax.sharding import PartitionSpec as P

SRC = 16
STEPS = 4
LAGS = 128
LANES = 128


def lag_rows(bin_count, lag_count, window_count):
    bins = np.arange(bin_count, dtype=np.int64)[None, :]
    offsets = np.arange(lag_count, dtype=np.int64)[:, None] - lag_count // 2
    phase = (bins * offsets % (2 * bin_count)) * (np.pi / bin_count)
    weight = np.where(bins == 0, 1.0, 2.0) / np.sqrt(2.0 * bin_count * window_count)
    rows = np.concatenate([weight * np.cos(phase), -weight * np.sin(phase)], 0)
    return rows.astype(np.float32).astype(jnp.bfloat16)


def prepare_kernel(blocks_ref, spectra_ref, laid_ref, *, run):
    terms = 2 * spectra_ref.shape[0]
    bins = spectra_ref.shape[3]
    steps, _, sources, _ = laid_ref.shape
    block = lax.broadcasted_iota(jnp.int32, (sources, LANES), 1) // run

    def chunk_step(q, carry):
        at = pl.ds(pl.multiple_of(q * LANES, LANES), LANES)
        for step in range(steps):
            first = pl.ds(pl.multiple_of(blocks_ref[step] * sources, sources), sources)
            tiles = [
                spectra_ref[i // 2, i % 2, first, at].astype(jnp.float32) for i in range(terms)
            ]
            gap = terms // 2
            while gap:
                high = (block // gap) % 2 == 1
                for i in range(terms):
                    if (i // gap) % 2 == 0:
                        low_tile, high_tile = tiles[i], tiles[i + gap]
                        tiles[i] = jnp.where(
                            high, pltpu.roll(high_tile, gap * run, 1), low_tile
                        )
                        tiles[i + gap] = jnp.where(
                            high, high_tile, pltpu.roll(low_tile, LANES - gap * run, 1)
                        )
                gap //= 2
            for i in range(terms // 2):
                laid_ref[step, q * (terms // 2) + i] = jnp.concatenate(
                    tiles[2 * i : 2 * i + 2], 1
                ).astype(jnp.bfloat16)
        return carry

    lax.fori_loop(0, bins // LANES, chunk_step, 0)


def prepare(spectra, blocks, steps, sources, run):
    bins = spectra.shape[3]
    return pl.pallas_call(
        functools.partial(prepare_kernel, run=run),
        out_shape=jax.ShapeDtypeStruct(
            (steps, bins // (2 * run), sources, 2 * LANES), spectra.dtype
        ),
        in_specs=[
            pl.BlockSpec(memory_space=pltpu.SMEM),
            pl.BlockSpec(memory_space=pltpu.VMEM),
        ],
        out_specs=pl.BlockSpec(memory_space=pltpu.VMEM),
        compiler_params=pltpu.CompilerParams(vmem_limit_bytes=16 << 20),
    )(blocks, spectra)


def main_kernel(
    owners_ref, own_ref, spectra_ref, lag_ref, out_ref,
    recv, cross_spectra, made, arrived, got,
    from_core, half, from_cross, quarter, from_low, from_high, to_high, to_low,
    core_send, core_recv, cross_send, cross_recv, up_send, up_recv,
    down_send, down_recv, share_send, share_recv, last_send, last_recv,
    sum_send, sum_recv,
    *, length, members, run,
):
    steps, _, groups, sources, width = own_ref.shape
    windows, _, receivers, bins = spectra_ref.shape
    terms = 2 * windows
    kept = sources // members
    me = lax.axis_index("chan")
    win = lax.axis_index("win")
    line, cross, core = me // 4, (me // 2) % 2, me % 2
    core_peer = me + 1 - 2 * core
    cross_peer = me + 2 - 4 * cross
    mine = 2 * core + cross
    theirs = 2 * core + 1 - cross
    has_low, has_high = line > 0, line < length - 1
    near_low = line < length // 2

    def remote(src, dst, send, recv, peer):
        return pltpu.make_async_remote_copy(
            src_ref=src, dst_ref=dst, send_sem=send, recv_sem=recv,
            device_id={"chan": peer}, device_id_type=pl.DeviceIdType.MESH,
        )

    def to_core(s):
        part = own_ref.at[s, pl.ds(2 * (1 - core), 2)]
        return remote(part, from_core.at[s], core_send.at[s], core_recv.at[s], core_peer)

    def to_cross(s):
        return remote(
            half.at[s, 1 - cross], from_cross.at[s], cross_send.at[s], cross_recv.at[s],
            cross_peer,
        )

    def go_up(s):
        return remote(to_high.at[s], from_low.at[s], up_send.at[s], up_recv.at[s], me + 4)

    def go_down(s):
        return remote(to_low.at[s], from_high.at[s], down_send.at[s], down_recv.at[s], me - 4)

    def share(s):
        ref = got.at[s, mine]
        return remote(ref, ref, share_send.at[s], share_recv.at[s], cross_peer)

    def last(s, which, index):
        ref = got.at[s, index]
        return remote(ref, ref, last_send.at[s, which], last_recv.at[s, which], core_peer)

    def add_up(s, j):
        peer = (win + j) % members
        return pltpu.make_async_remote_copy(
            src_ref=made.at[s, pl.ds(peer * kept, kept)],
            dst_ref=arrived.at[s, j - 1],
            send_sem=sum_send.at[s, j - 1],
            recv_sem=sum_recv.at[s, j - 1],
            device_id={"win": peer},
            device_id_type=pl.DeviceIdType.MESH,
        )

    barrier = pltpu.get_barrier_semaphore()

    def greet(peer):
        pl.semaphore_signal(
            barrier, inc=1, device_id={"chan": peer}, device_id_type=pl.DeviceIdType.MESH
        )

    greet(core_peer)
    greet(cross_peer)
    for j in range(1, members):
        pl.semaphore_signal(
            barrier,
            inc=1,
            device_id={"win": (win + j) % members},
            device_id_type=pl.DeviceIdType.MESH,
        )

    @pl.when(has_low)
    def _():
        greet(me - 4)

    @pl.when(has_high)
    def _():
        greet(me + 4)

    pl.semaphore_wait(
        barrier, 1 + members + jnp.where(has_low, 1, 0) + jnp.where(has_high, 1, 0)
    )

    @pl.loop(0, steps)
    def _(s):
        to_core(s).start()

    @pl.loop(0, steps)
    def _(s):
        to_core(s).wait_recv()
        half[s] = lax.select(owners_ref[s] == me, own_ref[s, pl.ds(2 * core, 2)], from_core[s])
        to_cross(s).start()

    @pl.loop(0, bins // LANES)
    def _(q):
        at = pl.ds(pl.multiple_of(q * LANES, LANES), LANES)
        for w in range(windows):
            real = spectra_ref[w, 0, :, at].astype(jnp.float32)
            imag = spectra_ref[w, 1, :, at].astype(jnp.float32)
            recv[2 * w, at, :] = jnp.concatenate([real, -imag], 0).T.astype(jnp.bfloat16)
            recv[2 * w + 1, at, :] = jnp.concatenate([imag, real], 0).T.astype(jnp.bfloat16)

    lane = lax.broadcasted_iota(jnp.int32, (run, width), 1) % run
    row = lax.broadcasted_iota(jnp.int32, (run, width), 0)
    keep = (lane == row).astype(jnp.float32)
    zero = jnp.zeros((LANES, LANES), jnp.bfloat16)

    def cross_part(s, part):
        def group_step(g, carry):
            base = pl.multiple_of((part * groups + g) * 2 * run, 2 * run)
            first = jnp.concatenate([recv[i, pl.ds(base, run), :] for i in range(terms)], 0)
            second = jnp.concatenate(
                [recv[i, pl.ds(base + run, run), :] for i in range(terms)], 0
            )
            weight = jnp.concatenate(
                [jnp.concatenate([first, zero], 1), jnp.concatenate([zero, second], 1)], 0
            )
            values = got[s, part, g].astype(jnp.float32)
            rows = jnp.concatenate(
                [
                    (jnp.broadcast_to(values[i : i + 1], (run, width)) * keep).astype(
                        jnp.bfloat16
                    )
                    for i in range(sources)
                ],
                0,
            )
            dots = jnp.dot(rows, weight, preferred_element_type=jnp.float32)
            dots = dots.astype(jnp.bfloat16)
            for i in range(sources):
                one = dots[i * run : (i + 1) * run]
                at = slice(i * LANES, (i + 1) * LANES)
                cross_spectra[s, pl.ds(base, run), at] = one[:, :LANES]
                cross_spectra[s, pl.ds(base + run, run), at] = one[:, LANES:]
            return carry

        lax.fori_loop(0, groups, group_step, 0, unroll=2)

    def lag_part(s):
        for pair in range(sources // 2):
            block = jnp.dot(
                lag_ref[...],
                cross_spectra[s, :, pair * 2 * LANES : (pair + 1) * 2 * LANES],
                preferred_element_type=jnp.float32,
            )
            turned = block.T
            lags = turned.shape[1] // 2
            for k in range(2):
                top = k * LANES
                made[s, 2 * pair + k] = (
                    turned[top : top + receivers, :lags]
                    + turned[top + receivers : top + 2 * receivers, lags:]
                )

    def low_side(s):
        @pl.when(has_low)
        def _():
            go_up(s).wait_recv()
            to_high[s] = lax.select(owners_ref[s] // 4 == line, quarter[s], from_low[s])

            @pl.when(has_high)
            def _():
                go_up(s).start()

    def high_side(s):
        @pl.when(has_high)
        def _():
            go_down(s).wait_recv()
            to_low[s] = lax.select(owners_ref[s] // 4 == line, quarter[s], from_high[s])

            @pl.when(has_low)
            def _():
                go_down(s).start()

    def enter(s):
        to_cross(s).wait_recv()
        value = lax.select((owners_ref[s] // 2) % 2 == cross, half[s, cross], from_cross[s])
        quarter[s] = value

        @pl.when(line == 0)
        def _():
            to_high[s] = value
            go_up(s).start()

        @pl.when(line == length - 1)
        def _():
            to_low[s] = value
            go_down(s).start()

    def near_side(s):
        @pl.when(near_low)
        def _():
            low_side(s)

        @pl.when(jnp.logical_not(near_low))
        def _():
            high_side(s)

    def far_side(s):
        @pl.when(near_low)
        def _():
            high_side(s)

        @pl.when(jnp.logical_not(near_low))
        def _():
            low_side(s)

        got[s, mine] = lax.select(owners_ref[s] // 4 <= line, to_high[s], to_low[s])
        share(s).start()
        last(s, 0, mine).start()

    def pass_on(s):
        share(s).wait_recv()
        last(s, 1, theirs).start()

    @pl.loop(0, steps + 2)
    def _(t):
        @pl.when(t < steps)
        def _():
            enter(t)

        @pl.when((t >= 1) & (t <= steps))
        def _():
            near_side(t - 1)

        @pl.when(t >= 2)
        def _():
            far_side(t - 2)

            @pl.when(t >= 3)
            def _():
                pass_on(t - 3)

            cross_part(t - 2, mine)

    pass_on(steps - 1)

    @pl.loop(0, steps)
    def _(s):
        cross_part(s, theirs)
        for which in range(2):
            last(s, which, mine).wait_recv()
        cross_part(s, 2 * (1 - core))
        cross_part(s, 2 * (1 - core) + 1)
        lag_part(s)
        for j in range(1, members):
            add_up(s, j).start()

    @pl.loop(0, steps)
    def _(s):
        to_core(s).wait_send()
        to_cross(s).wait_send()
        share(s).wait_send()
        for which in range(2):
            last(s, which, mine).wait_send()

        @pl.when(has_high)
        def _():
            go_up(s).wait_send()

        @pl.when(has_low)
        def _():
            go_down(s).wait_send()

        total = made[s, pl.ds(win * kept, kept)]
        for j in range(1, members):
            add_up(s, j).wait()
            total += arrived[s, j - 1]
        out_ref[s] = total


def main(laid, spectra, table, owners, run):
    steps, groups, sources, width = laid.shape
    windows, _, receivers, bins = spectra.shape
    members = lax.axis_size("win")
    lags = table.shape[0] // 2
    dtype = laid.dtype
    piece = (groups // 4, sources, width)
    kept = (sources // members, receivers, lags)
    return pl.pallas_call(
        functools.partial(
            main_kernel, length=lax.axis_size("chan") // 4, members=members, run=run
        ),
        out_shape=jax.ShapeDtypeStruct((steps,) + kept, jnp.float32),
        in_specs=[pl.BlockSpec(memory_space=pltpu.SMEM)]
        + [pl.BlockSpec(memory_space=pltpu.VMEM)] * 3,
        out_specs=pl.BlockSpec(memory_space=pltpu.VMEM),
        scratch_shapes=[
            pltpu.VMEM((2 * windows, bins, 2 * receivers), dtype),
            pltpu.VMEM((steps, bins, sources * LANES), dtype),
            pltpu.VMEM((steps, sources, receivers, lags), jnp.float32),
            pltpu.VMEM((steps, members - 1) + kept, jnp.float32),
            pltpu.VMEM((steps, 4) + piece, dtype),
            pltpu.VMEM((steps, 2) + piece, dtype),
            pltpu.VMEM((steps, 2) + piece, dtype),
        ]
        + [pltpu.VMEM((steps,) + piece, dtype)] * 6
        + [pltpu.SemaphoreType.DMA((steps,))] * 10
        + [pltpu.SemaphoreType.DMA((steps, 2))] * 2
        + [pltpu.SemaphoreType.DMA((steps, members - 1))] * 2,
        compiler_params=pltpu.CompilerParams(
            collective_id=0, has_side_effects=True, vmem_limit_bytes=60 << 20
        ),
    )(owners, laid.reshape((steps, 4) + piece), spectra, table)


def body(spectra, owners, blocks, max_lag):
    window_count, _, _, bin_count = spectra.shape
    group_count = lax.axis_size("win")
    run = LANES // (2 * window_count)
    table = jnp.asarray(lag_rows(bin_count, LAGS, window_count * group_count))
    turned = spectra.transpose(0, 2, 1, 3)
    laid = prepare(turned, blocks, STEPS, SRC, run)
    stacked = main(laid, turned, table, owners, run)
    offsets = jnp.abs(jnp.arange(LAGS, dtype=jnp.int32) - LAGS // 2)
    inside = offsets[None, None, None, :] <= max_lag[:, :, :, None]
    return jnp.where(inside, stacked, jnp.float32(0.0))


def solution(mesh):
    return jax.shard_map(
        body,
        mesh=mesh,
        in_specs=(P("win", "chan", None, None), P(), P(), P(None, "win", "chan")),
        out_specs=P(None, "win", "chan", None),
        check_vma=False,
    )
```

```python
import functools

import jax
import jax.numpy as jnp
import numpy as np
from jax import lax
from jax.experimental import pallas as pl
from jax.experimental.pallas import tpu as pltpu
from jax.sharding import PartitionSpec as P

SRC = 16
STEPS = 4
LAGS = 128
LANES = 128


def lag_rows(bin_count, lag_count, window_count):
    bins = np.arange(bin_count, dtype=np.int64)[None, :]
    offsets = np.arange(lag_count, dtype=np.int64)[:, None] - lag_count // 2
    phase = (bins * offsets % (2 * bin_count)) * (np.pi / bin_count)
    weight = np.where(bins == 0, 1.0, 2.0) / np.sqrt(2.0 * bin_count * window_count)
    rows = np.concatenate([weight * np.cos(phase), -weight * np.sin(phase)], 0)
    return rows.astype(np.float32).astype(jnp.bfloat16)


def prepare_kernel(blocks_ref, spectra_ref, laid_ref, *, run):
    terms = 2 * spectra_ref.shape[0]
    bins = spectra_ref.shape[3]
    steps, _, sources, _ = laid_ref.shape
    block = lax.broadcasted_iota(jnp.int32, (sources, LANES), 1) // run

    def chunk_step(q, carry):
        at = pl.ds(pl.multiple_of(q * LANES, LANES), LANES)
        for step in range(steps):
            first = pl.ds(pl.multiple_of(blocks_ref[step] * sources, sources), sources)
            tiles = [
                spectra_ref[i // 2, i % 2, first, at].astype(jnp.float32) for i in range(terms)
            ]
            gap = terms // 2
            while gap:
                high = (block // gap) % 2 == 1
                for i in range(terms):
                    if (i // gap) % 2 == 0:
                        low_tile, high_tile = tiles[i], tiles[i + gap]
                        tiles[i] = jnp.where(
                            high, pltpu.roll(high_tile, gap * run, 1), low_tile
                        )
                        tiles[i + gap] = jnp.where(
                            high, high_tile, pltpu.roll(low_tile, LANES - gap * run, 1)
                        )
                gap //= 2
            for i in range(terms // 2):
                laid_ref[step, q * (terms // 2) + i] = jnp.concatenate(
                    tiles[2 * i : 2 * i + 2], 1
                ).astype(jnp.bfloat16)
        return carry

    lax.fori_loop(0, bins // LANES, chunk_step, 0)


def prepare(spectra, blocks, steps, sources, run):
    bins = spectra.shape[3]
    return pl.pallas_call(
        functools.partial(prepare_kernel, run=run),
        out_shape=jax.ShapeDtypeStruct(
            (steps, bins // (2 * run), sources, 2 * LANES), spectra.dtype
        ),
        in_specs=[
            pl.BlockSpec(memory_space=pltpu.SMEM),
            pl.BlockSpec(memory_space=pltpu.VMEM),
        ],
        out_specs=pl.BlockSpec(memory_space=pltpu.VMEM),
        compiler_params=pltpu.CompilerParams(vmem_limit_bytes=16 << 20),
    )(blocks, spectra)


def main_kernel(
    owners_ref, own_ref, spectra_ref, lag_ref, out_ref,
    recv, cross_spectra, made, arrived, got,
    from_core, half, from_cross, quarter, from_low, from_high, to_high, to_low,
    core_send, core_recv, cross_send, cross_recv, up_send, up_recv,
    down_send, down_recv, share_send, share_recv, last_send, last_recv,
    sum_send, sum_recv,
    *, length, members, run,
):
    steps, _, groups, sources, width = own_ref.shape
    windows, _, receivers, bins = spectra_ref.shape
    terms = 2 * windows
    kept = sources // members
    me = lax.axis_index("chan")
    win = lax.axis_index("win")
    line, cross, core = me // 4, (me // 2) % 2, me % 2
    core_peer = me + 1 - 2 * core
    cross_peer = me + 2 - 4 * cross
    mine = 2 * core + cross
    theirs = 2 * core + 1 - cross
    has_low, has_high = line > 0, line < length - 1
    near_low = line < length // 2

    def remote(src, dst, send, recv, peer):
        return pltpu.make_async_remote_copy(
            src_ref=src, dst_ref=dst, send_sem=send, recv_sem=recv,
            device_id={"chan": peer}, device_id_type=pl.DeviceIdType.MESH,
        )

    def to_core(s):
        part = own_ref.at[s, pl.ds(2 * (1 - core), 2)]
        return remote(part, from_core.at[s], core_send.at[s], core_recv.at[s], core_peer)

    def to_cross(s):
        return remote(
            half.at[s, 1 - cross], from_cross.at[s], cross_send.at[s], cross_recv.at[s],
            cross_peer,
        )

    def go_up(s):
        return remote(to_high.at[s], from_low.at[s], up_send.at[s], up_recv.at[s], me + 4)

    def go_down(s):
        return remote(to_low.at[s], from_high.at[s], down_send.at[s], down_recv.at[s], me - 4)

    def share(s):
        ref = got.at[s, mine]
        return remote(ref, ref, share_send.at[s], share_recv.at[s], cross_peer)

    def last(s, which, index):
        ref = got.at[s, index]
        return remote(ref, ref, last_send.at[s, which], last_recv.at[s, which], core_peer)

    def add_up(s, j):
        peer = (win + j) % members
        return pltpu.make_async_remote_copy(
            src_ref=made.at[s, pl.ds(peer * kept, kept)],
            dst_ref=arrived.at[s, j - 1],
            send_sem=sum_send.at[s, j - 1],
            recv_sem=sum_recv.at[s, j - 1],
            device_id={"win": peer},
            device_id_type=pl.DeviceIdType.MESH,
        )

    barrier = pltpu.get_barrier_semaphore()

    def greet(peer):
        pl.semaphore_signal(
            barrier, inc=1, device_id={"chan": peer}, device_id_type=pl.DeviceIdType.MESH
        )

    greet(core_peer)
    greet(cross_peer)
    for j in range(1, members):
        pl.semaphore_signal(
            barrier,
            inc=1,
            device_id={"win": (win + j) % members},
            device_id_type=pl.DeviceIdType.MESH,
        )

    @pl.when(has_low)
    def _():
        greet(me - 4)

    @pl.when(has_high)
    def _():
        greet(me + 4)

    pl.semaphore_wait(
        barrier, 1 + members + jnp.where(has_low, 1, 0) + jnp.where(has_high, 1, 0)
    )

    @pl.loop(0, steps)
    def _(s):
        to_core(s).start()

    @pl.loop(0, steps)
    def _(s):
        to_core(s).wait_recv()
        half[s] = lax.select(owners_ref[s] == me, own_ref[s, pl.ds(2 * core, 2)], from_core[s])

        @pl.when(s < 2)
        def _():
            to_cross(s).start()

    @pl.loop(0, bins // LANES)
    def _(q):
        at = pl.ds(pl.multiple_of(q * LANES, LANES), LANES)
        for w in range(windows):
            real = spectra_ref[w, 0, :, at].astype(jnp.float32)
            imag = spectra_ref[w, 1, :, at].astype(jnp.float32)
            recv[2 * w, at, :] = jnp.concatenate([real, -imag], 0).T.astype(jnp.bfloat16)
            recv[2 * w + 1, at, :] = jnp.concatenate([imag, real], 0).T.astype(jnp.bfloat16)

    lane = lax.broadcasted_iota(jnp.int32, (run, width), 1) % run
    row = lax.broadcasted_iota(jnp.int32, (run, width), 0)
    keep = (lane == row).astype(jnp.float32)
    zero = jnp.zeros((LANES, LANES), jnp.bfloat16)

    def cross_part(s, part):
        def group_step(g, carry):
            base = pl.multiple_of((part * groups + g) * 2 * run, 2 * run)
            first = jnp.concatenate([recv[i, pl.ds(base, run), :] for i in range(terms)], 0)
            second = jnp.concatenate(
                [recv[i, pl.ds(base + run, run), :] for i in range(terms)], 0
            )
            weight = jnp.concatenate(
                [jnp.concatenate([first, zero], 1), jnp.concatenate([zero, second], 1)], 0
            )
            values = got[s, part, g].astype(jnp.float32)
            rows = jnp.concatenate(
                [
                    (jnp.broadcast_to(values[i : i + 1], (run, width)) * keep).astype(
                        jnp.bfloat16
                    )
                    for i in range(sources)
                ],
                0,
            )
            dots = jnp.dot(rows, weight, preferred_element_type=jnp.float32)
            dots = dots.astype(jnp.bfloat16)
            for i in range(sources):
                one = dots[i * run : (i + 1) * run]
                at = slice(i * LANES, (i + 1) * LANES)
                cross_spectra[s, pl.ds(base, run), at] = one[:, :LANES]
                cross_spectra[s, pl.ds(base + run, run), at] = one[:, LANES:]
            return carry

        lax.fori_loop(0, groups, group_step, 0, unroll=2)

    def lag_part(s):
        for j in list(range(1, members)) + [0]:
            for p in range(kept // 2):
                pair = ((win + j) % members) * (kept // 2) + p
                at = pl.ds(pl.multiple_of(pair * 2 * LANES, 2 * LANES), 2 * LANES)
                block = jnp.dot(
                    lag_ref[...], cross_spectra[s, :, at], preferred_element_type=jnp.float32
                )
                turned = block.T
                lags = turned.shape[1] // 2
                for k in range(2):
                    top = k * LANES
                    made[s, 2 * pair + k] = (
                        turned[top : top + receivers, :lags]
                        + turned[top + receivers : top + 2 * receivers, lags:]
                    )
            if j > 0:
                add_up(s, j).start()

    def low_side(s):
        @pl.when(has_low)
        def _():
            go_up(s).wait_recv()
            to_high[s] = lax.select(owners_ref[s] // 4 == line, quarter[s], from_low[s])

            @pl.when(has_high)
            def _():
                go_up(s).start()

    def high_side(s):
        @pl.when(has_high)
        def _():
            go_down(s).wait_recv()
            to_low[s] = lax.select(owners_ref[s] // 4 == line, quarter[s], from_high[s])

            @pl.when(has_low)
            def _():
                go_down(s).start()

    def enter(s):
        to_cross(s).wait_recv()

        @pl.when(s + 2 < steps)
        def _():
            to_cross(s + 2).start()

        value = lax.select((owners_ref[s] // 2) % 2 == cross, half[s, cross], from_cross[s])
        quarter[s] = value

        @pl.when(line == 0)
        def _():
            to_high[s] = value
            go_up(s).start()

        @pl.when(line == length - 1)
        def _():
            to_low[s] = value
            go_down(s).start()

    def near_side(s):
        @pl.when(near_low)
        def _():
            low_side(s)

        @pl.when(jnp.logical_not(near_low))
        def _():
            high_side(s)

    def far_side(s):
        @pl.when(near_low)
        def _():
            high_side(s)

        @pl.when(jnp.logical_not(near_low))
        def _():
            low_side(s)

    inner = (line > 0) & (line < length - 1)

    def settle(s):
        @pl.when(jnp.logical_not(inner))
        def _():
            far_side(s)

        got[s, mine] = lax.select(owners_ref[s] // 4 <= line, to_high[s], to_low[s])
        share(s).start()
        last(s, 0, mine).start()

    def pass_on(s):
        share(s).wait_recv()
        last(s, 1, theirs).start()

    @pl.loop(0, steps + 4)
    def _(t):
        @pl.when(t >= 4)
        def _():
            pass_on(t - 4)

        @pl.when((t >= 3) & (t < steps + 3))
        def _():
            settle(t - 3)

        @pl.when((t >= 2) & (t < steps + 2) & inner)
        def _():
            far_side(t - 2)

        @pl.when((t >= 1) & (t < steps + 1))
        def _():
            near_side(t - 1)

        @pl.when(t < steps)
        def _():
            enter(t)

        @pl.when((t >= 3) & (t < steps + 3))
        def _():
            cross_part(t - 3, mine)

        @pl.when(t >= 4)
        def _():
            s = t - 4
            cross_part(s, theirs)
            for which in range(2):
                last(s, which, mine).wait_recv()
            cross_part(s, 2 * (1 - core))
            cross_part(s, 2 * (1 - core) + 1)
            lag_part(s)

    @pl.loop(0, steps)
    def _(s):
        to_core(s).wait_send()
        to_cross(s).wait_send()
        share(s).wait_send()
        for which in range(2):
            last(s, which, mine).wait_send()

        @pl.when(has_high)
        def _():
            go_up(s).wait_send()

        @pl.when(has_low)
        def _():
            go_down(s).wait_send()

        total = made[s, pl.ds(win * kept, kept)]
        for j in range(1, members):
            add_up(s, j).wait()
            total += arrived[s, j - 1]
        out_ref[s] = total


def main(laid, spectra, table, owners, run):
    steps, groups, sources, width = laid.shape
    windows, _, receivers, bins = spectra.shape
    members = lax.axis_size("win")
    lags = table.shape[0] // 2
    dtype = laid.dtype
    piece = (groups // 4, sources, width)
    kept = (sources // members, receivers, lags)
    return pl.pallas_call(
        functools.partial(
            main_kernel, length=lax.axis_size("chan") // 4, members=members, run=run
        ),
        out_shape=jax.ShapeDtypeStruct((steps,) + kept, jnp.float32),
        in_specs=[pl.BlockSpec(memory_space=pltpu.SMEM)]
        + [pl.BlockSpec(memory_space=pltpu.VMEM)] * 3,
        out_specs=pl.BlockSpec(memory_space=pltpu.VMEM),
        scratch_shapes=[
            pltpu.VMEM((2 * windows, bins, 2 * receivers), dtype),
            pltpu.VMEM((steps, bins, sources * LANES), dtype),
            pltpu.VMEM((steps, sources, receivers, lags), jnp.float32),
            pltpu.VMEM((steps, members - 1) + kept, jnp.float32),
            pltpu.VMEM((steps, 4) + piece, dtype),
            pltpu.VMEM((steps, 2) + piece, dtype),
            pltpu.VMEM((steps, 2) + piece, dtype),
        ]
        + [pltpu.VMEM((steps,) + piece, dtype)] * 6
        + [pltpu.SemaphoreType.DMA((steps,))] * 10
        + [pltpu.SemaphoreType.DMA((steps, 2))] * 2
        + [pltpu.SemaphoreType.DMA((steps, members - 1))] * 2,
        compiler_params=pltpu.CompilerParams(
            collective_id=0, has_side_effects=True, vmem_limit_bytes=60 << 20
        ),
    )(owners, laid.reshape((steps, 4) + piece), spectra, table)


def body(spectra, owners, blocks, max_lag):
    window_count, _, _, bin_count = spectra.shape
    group_count = lax.axis_size("win")
    run = LANES // (2 * window_count)
    table = jnp.asarray(lag_rows(bin_count, LAGS, window_count * group_count))
    turned = spectra.transpose(0, 2, 1, 3)
    laid = prepare(turned, blocks, STEPS, SRC, run)
    stacked = main(laid, turned, table, owners, run)
    offsets = jnp.abs(jnp.arange(LAGS, dtype=jnp.int32) - LAGS // 2)
    inside = offsets[None, None, None, :] <= max_lag[:, :, :, None]
    return jnp.where(inside, stacked, jnp.float32(0.0))


def solution(mesh):
    return jax.shard_map(
        body,
        mesh=mesh,
        in_specs=(P("win", "chan", None, None), P(), P(), P(None, "win", "chan")),
        out_specs=P(None, "win", "chan", None),
        check_vma=False,
    )
```

```python
import functools

import jax
import jax.numpy as jnp
import numpy as np
from jax import lax
from jax.experimental import pallas as pl
from jax.experimental.pallas import tpu as pltpu
from jax.sharding import PartitionSpec as P

SRC = 16
STEPS = 4
LAGS = 128
LANES = 128


def lag_rows(bin_count, lag_count, window_count):
    bins = np.arange(bin_count, dtype=np.int64)[None, :]
    offsets = np.arange(lag_count, dtype=np.int64)[:, None] - lag_count // 2
    phase = (bins * offsets % (2 * bin_count)) * (np.pi / bin_count)
    weight = np.where(bins == 0, 1.0, 2.0) / np.sqrt(2.0 * bin_count * window_count)
    rows = np.concatenate([weight * np.cos(phase), -weight * np.sin(phase)], 0)
    return rows.astype(np.float32).astype(jnp.bfloat16)


def prepare_kernel(blocks_ref, spectra_ref, laid_ref, *, run):
    terms = 2 * spectra_ref.shape[0]
    bins = spectra_ref.shape[3]
    steps, _, sources, _ = laid_ref.shape
    block = lax.broadcasted_iota(jnp.int32, (sources, LANES), 1) // run

    def chunk_step(q, carry):
        at = pl.ds(pl.multiple_of(q * LANES, LANES), LANES)
        for step in range(steps):
            first = pl.ds(pl.multiple_of(blocks_ref[step] * sources, sources), sources)
            tiles = [
                spectra_ref[i // 2, i % 2, first, at].astype(jnp.float32) for i in range(terms)
            ]
            gap = terms // 2
            while gap:
                high = (block // gap) % 2 == 1
                for i in range(terms):
                    if (i // gap) % 2 == 0:
                        low_tile, high_tile = tiles[i], tiles[i + gap]
                        tiles[i] = jnp.where(
                            high, pltpu.roll(high_tile, gap * run, 1), low_tile
                        )
                        tiles[i + gap] = jnp.where(
                            high, high_tile, pltpu.roll(low_tile, LANES - gap * run, 1)
                        )
                gap //= 2
            for i in range(terms // 2):
                laid_ref[step, q * (terms // 2) + i] = jnp.concatenate(
                    tiles[2 * i : 2 * i + 2], 1
                ).astype(jnp.bfloat16)
        return carry

    lax.fori_loop(0, bins // LANES, chunk_step, 0)


def prepare(spectra, blocks, steps, sources, run):
    bins = spectra.shape[3]
    return pl.pallas_call(
        functools.partial(prepare_kernel, run=run),
        out_shape=jax.ShapeDtypeStruct(
            (steps, bins // (2 * run), sources, 2 * LANES), spectra.dtype
        ),
        in_specs=[
            pl.BlockSpec(memory_space=pltpu.SMEM),
            pl.BlockSpec(memory_space=pltpu.VMEM),
        ],
        out_specs=pl.BlockSpec(memory_space=pltpu.VMEM),
        compiler_params=pltpu.CompilerParams(vmem_limit_bytes=16 << 20),
    )(blocks, spectra)


def main_kernel(
    owners_ref, own_ref, spectra_ref, lag_ref, out_ref,
    recv, cross_spectra, made, arrived, got,
    from_core, half, from_cross, quarter, from_low, from_high, to_high, to_low,
    core_send, core_recv, cross_send, cross_recv, up_send, up_recv,
    down_send, down_recv, share_send, share_recv, last_send, last_recv,
    sum_send, sum_recv,
    *, length, members, run,
):
    steps, _, groups, sources, width = own_ref.shape
    windows, _, receivers, bins = spectra_ref.shape
    terms = 2 * windows
    kept = sources // members
    me = lax.axis_index("chan")
    win = lax.axis_index("win")
    line, cross, core = me // 4, (me // 2) % 2, me % 2
    core_peer = me + 1 - 2 * core
    cross_peer = me + 2 - 4 * cross
    mine = 2 * core + cross
    theirs = 2 * core + 1 - cross
    has_low, has_high = line > 0, line < length - 1
    near_low = line < length // 2

    def remote(src, dst, send, recv, peer):
        return pltpu.make_async_remote_copy(
            src_ref=src, dst_ref=dst, send_sem=send, recv_sem=recv,
            device_id={"chan": peer}, device_id_type=pl.DeviceIdType.MESH,
        )

    def to_core(s):
        part = own_ref.at[s, pl.ds(2 * (1 - core), 2)]
        return remote(part, from_core.at[s], core_send.at[s], core_recv.at[s], core_peer)

    def to_cross(s):
        return remote(
            half.at[s, 1 - cross], from_cross.at[s], cross_send.at[s], cross_recv.at[s],
            cross_peer,
        )

    def go_up(s):
        return remote(to_high.at[s], from_low.at[s], up_send.at[s], up_recv.at[s], me + 4)

    def go_down(s):
        return remote(to_low.at[s], from_high.at[s], down_send.at[s], down_recv.at[s], me - 4)

    def share(s):
        ref = got.at[s, mine]
        return remote(ref, ref, share_send.at[s], share_recv.at[s], cross_peer)

    def last(s, which, index):
        ref = got.at[s, index]
        return remote(ref, ref, last_send.at[s, which], last_recv.at[s, which], core_peer)

    def add_up(s, j):
        peer = (win + j) % members
        return pltpu.make_async_remote_copy(
            src_ref=made.at[s, pl.ds(peer * kept, kept)],
            dst_ref=arrived.at[s, j - 1],
            send_sem=sum_send.at[s, j - 1],
            recv_sem=sum_recv.at[s, j - 1],
            device_id={"win": peer},
            device_id_type=pl.DeviceIdType.MESH,
        )

    barrier = pltpu.get_barrier_semaphore()

    def greet(peer):
        pl.semaphore_signal(
            barrier, inc=1, device_id={"chan": peer}, device_id_type=pl.DeviceIdType.MESH
        )

    greet(core_peer)
    greet(cross_peer)
    for j in range(1, members):
        pl.semaphore_signal(
            barrier,
            inc=1,
            device_id={"win": (win + j) % members},
            device_id_type=pl.DeviceIdType.MESH,
        )

    @pl.when(has_low)
    def _():
        greet(me - 4)

    @pl.when(has_high)
    def _():
        greet(me + 4)

    pl.semaphore_wait(
        barrier, 1 + members + jnp.where(has_low, 1, 0) + jnp.where(has_high, 1, 0)
    )

    @pl.loop(0, steps)
    def _(s):
        to_core(s).start()

    @pl.loop(0, steps)
    def _(s):
        to_core(s).wait_recv()
        half[s] = lax.select(owners_ref[s] == me, own_ref[s, pl.ds(2 * core, 2)], from_core[s])

        @pl.when(s < 2)
        def _():
            to_cross(s).start()

    @pl.loop(0, bins // LANES)
    def _(q):
        at = pl.ds(pl.multiple_of(q * LANES, LANES), LANES)
        for w in range(windows):
            real = spectra_ref[w, 0, :, at].astype(jnp.float32)
            imag = spectra_ref[w, 1, :, at].astype(jnp.float32)
            recv[2 * w, at, :] = jnp.concatenate([real, -imag], 0).T.astype(jnp.bfloat16)
            recv[2 * w + 1, at, :] = jnp.concatenate([imag, real], 0).T.astype(jnp.bfloat16)

    lane = lax.broadcasted_iota(jnp.int32, (run, width), 1) % run
    row = lax.broadcasted_iota(jnp.int32, (run, width), 0)
    keep = (lane == row).astype(jnp.float32)
    zero = jnp.zeros((LANES, LANES), jnp.bfloat16)

    def cross_part(s, part):
        def group_step(g, carry):
            base = pl.multiple_of((part * groups + g) * 2 * run, 2 * run)
            first = jnp.concatenate([recv[i, pl.ds(base, run), :] for i in range(terms)], 0)
            second = jnp.concatenate(
                [recv[i, pl.ds(base + run, run), :] for i in range(terms)], 0
            )
            weight = jnp.concatenate(
                [jnp.concatenate([first, zero], 1), jnp.concatenate([zero, second], 1)], 0
            )
            values = got[s, part, g].astype(jnp.float32)
            rows = jnp.concatenate(
                [
                    (jnp.broadcast_to(values[i : i + 1], (run, width)) * keep).astype(
                        jnp.bfloat16
                    )
                    for i in range(sources)
                ],
                0,
            )
            dots = jnp.dot(rows, weight, preferred_element_type=jnp.float32)
            dots = dots.astype(jnp.bfloat16)
            for i in range(sources):
                one = dots[i * run : (i + 1) * run]
                at = slice(i * LANES, (i + 1) * LANES)
                cross_spectra[s, pl.ds(base, run), at] = one[:, :LANES]
                cross_spectra[s, pl.ds(base + run, run), at] = one[:, LANES:]
            return carry

        lax.fori_loop(0, groups, group_step, 0, unroll=8)

    def lag_part(s):
        for j in list(range(1, members)) + [0]:
            for p in range(kept // 2):
                pair = ((win + j) % members) * (kept // 2) + p
                at = pl.ds(pl.multiple_of(pair * 2 * LANES, 2 * LANES), 2 * LANES)
                block = jnp.dot(
                    lag_ref[...], cross_spectra[s, :, at], preferred_element_type=jnp.float32
                )
                turned = block.T
                lags = turned.shape[1] // 2
                for k in range(2):
                    top = k * LANES
                    made[s, 2 * pair + k] = (
                        turned[top : top + receivers, :lags]
                        + turned[top + receivers : top + 2 * receivers, lags:]
                    )
            if j > 0:
                add_up(s, j).start()

    def low_side(s):
        @pl.when(has_low)
        def _():
            go_up(s).wait_recv()
            to_high[s] = lax.select(owners_ref[s] // 4 == line, quarter[s], from_low[s])

            @pl.when(has_high)
            def _():
                go_up(s).start()

    def high_side(s):
        @pl.when(has_high)
        def _():
            go_down(s).wait_recv()
            to_low[s] = lax.select(owners_ref[s] // 4 == line, quarter[s], from_high[s])

            @pl.when(has_low)
            def _():
                go_down(s).start()

    def enter(s):
        to_cross(s).wait_recv()

        @pl.when(s + 2 < steps)
        def _():
            to_cross(s + 2).start()

        value = lax.select((owners_ref[s] // 2) % 2 == cross, half[s, cross], from_cross[s])
        quarter[s] = value

        @pl.when(line == 0)
        def _():
            to_high[s] = value
            go_up(s).start()

        @pl.when(line == length - 1)
        def _():
            to_low[s] = value
            go_down(s).start()

    def near_side(s):
        @pl.when(near_low)
        def _():
            low_side(s)

        @pl.when(jnp.logical_not(near_low))
        def _():
            high_side(s)

    def far_side(s):
        @pl.when(near_low)
        def _():
            high_side(s)

        @pl.when(jnp.logical_not(near_low))
        def _():
            low_side(s)

    inner = (line > 0) & (line < length - 1)

    def settle(s):
        @pl.when(jnp.logical_not(inner))
        def _():
            far_side(s)

        got[s, mine] = lax.select(owners_ref[s] // 4 <= line, to_high[s], to_low[s])
        share(s).start()
        last(s, 0, mine).start()

    def pass_on(s):
        share(s).wait_recv()
        last(s, 1, theirs).start()

    @pl.loop(0, steps + 4)
    def _(t):
        @pl.when(t >= 4)
        def _():
            pass_on(t - 4)

        @pl.when((t >= 3) & (t < steps + 3))
        def _():
            settle(t - 3)

        @pl.when((t >= 2) & (t < steps + 2) & inner)
        def _():
            far_side(t - 2)

        @pl.when((t >= 1) & (t < steps + 1))
        def _():
            near_side(t - 1)

        @pl.when(t < steps)
        def _():
            enter(t)

        @pl.when((t >= 3) & (t < steps + 3))
        def _():
            cross_part(t - 3, mine)

        @pl.when(t >= 4)
        def _():
            s = t - 4
            cross_part(s, theirs)
            for which in range(2):
                last(s, which, mine).wait_recv()
            cross_part(s, 2 * (1 - core))
            cross_part(s, 2 * (1 - core) + 1)
            lag_part(s)

    @pl.loop(0, steps)
    def _(s):
        to_core(s).wait_send()
        to_cross(s).wait_send()
        share(s).wait_send()
        for which in range(2):
            last(s, which, mine).wait_send()

        @pl.when(has_high)
        def _():
            go_up(s).wait_send()

        @pl.when(has_low)
        def _():
            go_down(s).wait_send()

        total = made[s, pl.ds(win * kept, kept)]
        for j in range(1, members):
            add_up(s, j).wait()
            total += arrived[s, j - 1]
        out_ref[s] = total


def main(laid, spectra, table, owners, run):
    steps, groups, sources, width = laid.shape
    windows, _, receivers, bins = spectra.shape
    members = lax.axis_size("win")
    lags = table.shape[0] // 2
    dtype = laid.dtype
    piece = (groups // 4, sources, width)
    kept = (sources // members, receivers, lags)
    return pl.pallas_call(
        functools.partial(
            main_kernel, length=lax.axis_size("chan") // 4, members=members, run=run
        ),
        out_shape=jax.ShapeDtypeStruct((steps,) + kept, jnp.float32),
        in_specs=[pl.BlockSpec(memory_space=pltpu.SMEM)]
        + [pl.BlockSpec(memory_space=pltpu.VMEM)] * 3,
        out_specs=pl.BlockSpec(memory_space=pltpu.VMEM),
        scratch_shapes=[
            pltpu.VMEM((2 * windows, bins, 2 * receivers), dtype),
            pltpu.VMEM((steps, bins, sources * LANES), dtype),
            pltpu.VMEM((steps, sources, receivers, lags), jnp.float32),
            pltpu.VMEM((steps, members - 1) + kept, jnp.float32),
            pltpu.VMEM((steps, 4) + piece, dtype),
            pltpu.VMEM((steps, 2) + piece, dtype),
            pltpu.VMEM((steps, 2) + piece, dtype),
        ]
        + [pltpu.VMEM((steps,) + piece, dtype)] * 6
        + [pltpu.SemaphoreType.DMA((steps,))] * 10
        + [pltpu.SemaphoreType.DMA((steps, 2))] * 2
        + [pltpu.SemaphoreType.DMA((steps, members - 1))] * 2,
        compiler_params=pltpu.CompilerParams(
            collective_id=0, has_side_effects=True, vmem_limit_bytes=60 << 20
        ),
    )(owners, laid.reshape((steps, 4) + piece), spectra, table)


def body(spectra, owners, blocks, max_lag):
    window_count, _, _, bin_count = spectra.shape
    group_count = lax.axis_size("win")
    run = LANES // (2 * window_count)
    table = jnp.asarray(lag_rows(bin_count, LAGS, window_count * group_count))
    turned = spectra.transpose(0, 2, 1, 3)
    laid = prepare(turned, blocks, STEPS, SRC, run)
    stacked = main(laid, turned, table, owners, run)
    offsets = jnp.abs(jnp.arange(LAGS, dtype=jnp.int32) - LAGS // 2)
    inside = offsets[None, None, None, :] <= max_lag[:, :, :, None]
    return jnp.where(inside, stacked, jnp.float32(0.0))


def solution(mesh):
    return jax.shard_map(
        body,
        mesh=mesh,
        in_specs=(P("win", "chan", None, None), P(), P(), P(None, "win", "chan")),
        out_specs=P(None, "win", "chan", None),
        check_vma=False,
    )
```
